32 devices in a mesh: fsdp: 2 (over y), ctx: 4 (over x, core), tp: 4 (over z).
Axes of the slice: x: 2, y: 2, z: 4, core: 2. Of those that a mesh axis runs over, the one named last changes fastest.
Arguments:
- tokens: bfloat16 [4, 1024, 1024], P('fsdp', 'ctx'), may hold values from -6 to 6
- places: int32 [3, 4, 1024], P(None, 'fsdp', 'ctx'), may hold values from 0 to 15
- d_out: bfloat16 [4, 1024, 1024], P('fsdp', 'ctx'), may hold values from -6 to 6
- w_qkv: bfloat16 [3, 1024, 1024], P(None, 'fsdp', 'tp'), may hold values from -0.1875 to 0.1875
- b_qkv: bfloat16 [3, 16, 64], P(None, 'tp', 'fsdp'), may hold values from -3 to 3
- w_proj: bfloat16 [1024, 1024], P('tp', 'fsdp'), may hold values from -0.25 to 0.25
- b_proj: bfloat16 [1024], P('fsdp'), may hold values from -3 to 3
- ln1_gain: bfloat16 [1024], P('fsdp'), may hold values from 0.25 to 1.75
- ln1_shift: bfloat16 [1024], P('fsdp'), may hold values from -2 to 2
- ln2_gain: bfloat16 [1024], P('fsdp'), may hold values from 0.25 to 1.75
- ln2_shift: bfloat16 [1024], P('fsdp'), may hold values from -2 to 2
- w_fc1: bfloat16 [1024, 4096], P('fsdp', 'tp'), may hold values from -0.1875 to 0.1875
- b_fc1: bfloat16 [16, 256], P('tp', 'fsdp'), may hold values from -3 to 3
- w_fc2: bfloat16 [4096, 1024], P('tp', 'fsdp'), may hold values from -0.09375 to 0.09375
- b_fc2: bfloat16 [1024], P('fsdp'), may hold values from -3 to 3
Outputs:
- output: bfloat16 [4, 1024, 1024], P('fsdp', 'ctx')
- input_grad: bfloat16 [4, 1024, 1024], P('fsdp', 'ctx')
- grad_w_qkv: float32 [3, 1024, 1024], P(None, 'fsdp', 'tp')
- grad_b_qkv: float32 [3, 16, 64], P(None, 'tp', 'fsdp')
- grad_w_proj: float32 [1024, 1024], P('tp', 'fsdp')
- grad_b_proj: float32 [1024], P('fsdp')
- grad_ln1_gain: float32 [1024], P('fsdp')
- grad_ln1_shift: float32 [1024], P('fsdp')
- grad_ln2_gain: float32 [1024], P('fsdp')
- grad_ln2_shift: float32 [1024], P('fsdp')
- grad_w_fc1: float32 [1024, 4096], P('fsdp', 'tp')
- grad_b_fc1: float32 [16, 256], P('tp', 'fsdp')
- grad_w_fc2: float32 [4096, 1024], P('tp', 'fsdp')
- grad_b_fc2: float32 [1024], P('fsdp')
The draws below stay inside these ranges and needn't reach their ends.
Inputs may be any that keep to these rules, and one draw needn't show every extreme that they name: `places`: each token's grid coordinates: frame, row and column.
All inputs are finite; a program needn't handle non-finite values.
Results may differ from the reference program's by a relative error of at most 0.02.
Values may be sent and summed in bfloat16 or wider, within the bound.
No kernel may reach another device: no remote copies, remote signals or barrier semaphores. Data moves between devices by JAX's collectives and lax.ppermute only.
A program may use at most 128 MiB of HBM per device.

```python
import math
import jax
import jax.numpy as jnp
from jax import lax

D = 1024
H = 16
HD = 64
FF = 4096
LEN = 1024
CLIPS = 4
ROT_PAIRS = 10


def plant(array, own_key, smallest, top_value):
    place = [jax.random.randint(jax.random.fold_in(own_key, axis), (), 0, length) for axis, length in enumerate(array.shape)]
    longest = array.shape.index(max(array.shape))
    neighbour = place[:longest] + [(place[longest] + 1) % array.shape[longest]] + place[longest + 1:]
    return array.at[tuple(place)].set(smallest).at[tuple(neighbour)].set(top_value)


def block_levels(key, dims, split, smallest, largest):
    level = 1.0
    for dim, shards_of in split:
        draws = jax.random.uniform(jax.random.fold_in(jax.random.fold_in(key, 6), dim), (shards_of,), jnp.float32, smallest / len(split), largest / len(split))
        level = level * jnp.repeat(jnp.exp(draws), dims[dim] // shards_of).reshape((-1,) + (1,) * (len(dims) - 1 - dim))
    return level


def bell_draw(own_key, shape, deviation, reach, pieces=(), dtype=jnp.bfloat16):
    drawn = deviation * jax.random.normal(own_key, shape, jnp.float32)
    if pieces:
        drawn = drawn * block_levels(own_key, shape, pieces, -0.22, 0.18)
    return jnp.clip(drawn, -reach, reach).astype(dtype)


def setup_inputs(seed: int = 0) -> dict:
    key_list = jax.random.split(jax.random.key(seed), 16)
    return {
        "tokens": bell_draw(key_list[0], (CLIPS, LEN, D), 1.0, 6.0, ((0, 2), (1, 4))),
        "places": plant(jax.random.randint(key_list[1], (3, CLIPS, LEN), 0, 16), jax.random.fold_in(key_list[1], 1), 0, 15).astype(jnp.int32),
        "d_out": bell_draw(key_list[2], (CLIPS, LEN, D), 1.0, 6.0, ((0, 2), (1, 4))),
        "w_qkv": bell_draw(key_list[3], (3, D, D), D ** -0.5, 0.1875, ((1, 2), (2, 4))),
        "b_qkv": bell_draw(key_list[4], (3, H, HD), 0.5, 3.0, ((1, 4), (2, 2))),
        "w_proj": bell_draw(key_list[5], (D, D), (D // 2) ** -0.5, 0.25, ((0, 4), (1, 2))),
        "b_proj": bell_draw(key_list[6], (D,), 0.5, 3.0, ((0, 2),)),
        "ln1_gain": jnp.clip(1.0 + 0.15 * jax.random.normal(key_list[7], (D,), jnp.float32), 0.25, 1.75).astype(jnp.bfloat16),
        "ln1_shift": bell_draw(key_list[8], (D,), 0.3, 2.0, ((0, 2),)),
        "ln2_gain": jnp.clip(1.0 + 0.15 * jax.random.normal(key_list[9], (D,), jnp.float32), 0.25, 1.75).astype(jnp.bfloat16),
        "ln2_shift": bell_draw(key_list[10], (D,), 0.3, 2.0, ((0, 2),)),
        "w_fc1": bell_draw(key_list[11], (D, FF), D ** -0.5, 0.1875, ((0, 2), (1, 4))),
        "b_fc1": bell_draw(key_list[12], (H, FF // H), 0.5, 3.0, ((0, 4), (1, 2))),
        "w_fc2": bell_draw(key_list[13], (FF, D), FF ** -0.5, 0.09375, ((0, 4), (1, 2))),
        "b_fc2": bell_draw(key_list[14], (D,), 0.5, 3.0, ((0, 2),)),
    }


@jax.custom_vjp
def low(v):
    return lax.optimization_barrier(v.astype(jnp.bfloat16)).astype(jnp.float32)

@jax.custom_vjp
def low_back(v):
    return v

def low_keep(v):
    return (low(v), None)

def low_pass(kept, grad):
    return (grad,)

def back_keep(v):
    return (v, None)

def back_low(kept, grad):
    return (low(grad),)
low.defvjp(low_keep, low_pass)
low_back.defvjp(back_keep, back_low)
norm_epsilon = 1e-06

def layer_norm(values, gain_vector, shift_vector):
    centre = values - lax.optimization_barrier(jnp.mean(values, axis=-1, keepdims=True))
    spread = lax.optimization_barrier(jnp.mean(centre * centre, axis=-1, keepdims=True))
    return centre * lax.rsqrt(spread + norm_epsilon) * gain_vector + shift_vector

def rotary_tables(place_rows, head_size, pair_count):
    position_dim = jnp.arange(head_size)
    portion = position_dim // (2 * pair_count)
    within = position_dim % (2 * pair_count) // 2
    frequency = jnp.exp(within.astype(jnp.float32) * (-math.log(10000.0) / pair_count))
    angles = jnp.zeros((place_rows.shape[1], head_size), jnp.float32)
    for component in range(3):
        picked = jnp.where(portion == component, frequency, jnp.zeros_like(frequency))
        angles = angles + place_rows[component].astype(jnp.float32)[:, None] * picked[None, :]
    return (jnp.cos(angles), jnp.sin(angles))

def rotate(values, cosine_table, sine_table):
    paired = values.reshape(values.shape[:-1] + (values.shape[-1] // 2, 2))
    turned = jnp.stack((-paired[..., 1], paired[..., 0]), axis=-1).reshape(values.shape)
    return values * cosine_table[:, None, :] + turned * sine_table[:, None, :]

def block_forward(tokens_in, cosine_table, sine_table, weights):
    w_qkv, b_qkv, w_proj, b_proj, gain_one, shift_one, gain_two, shift_two, w_fc1, b_fc1, w_fc2, b_fc2 = weights
    highest = lax.Precision.HIGHEST
    score_scale = 1.0 / math.sqrt(HD)
    normed = low(layer_norm(tokens_in, gain_one, shift_one))
    projected = jnp.einsum('rd,jdc->jrc', normed, w_qkv, precision=highest) + b_qkv.reshape(3, 1, D)
    head_shape = (LEN, H, HD)
    query_rot = low(rotate(low_back(projected[0]).reshape(head_shape), cosine_table, sine_table))
    keys_rot = low(rotate(low_back(projected[1]).reshape(head_shape), cosine_table, sine_table))
    values_in = low(low_back(projected[2])).reshape(head_shape)
    scores = low_back(jnp.einsum('qhd,khd->hqk', query_rot, keys_rot, precision=highest) * score_scale)
    raised = jnp.exp(scores - lax.optimization_barrier(jnp.max(scores, axis=-1, keepdims=True)))
    soft_weights = low(raised / lax.optimization_barrier(jnp.sum(raised, axis=-1, keepdims=True)))
    attended = jnp.einsum('hqk,khd->qhd', soft_weights, values_in, precision=highest).reshape(LEN, D)
    attended = low_back(low(attended))
    middle = tokens_in + low_back(jnp.dot(attended, w_proj, precision=highest) + b_proj)
    normed_two = low(layer_norm(middle, gain_two, shift_two))
    hidden = low_back(jnp.dot(normed_two, w_fc1, precision=highest) + b_fc1.reshape(FF))
    active = low(jax.nn.gelu(hidden, approximate=False))
    return middle + low_back(jnp.dot(active, w_fc2, precision=highest) + b_fc2)

def reference(tokens, places, d_out, w_qkv, b_qkv, w_proj, b_proj, ln1_gain, ln1_shift, ln2_gain, ln2_shift, w_fc1, b_fc1, w_fc2, b_fc2):
    weights = tuple((member.astype(jnp.float32) for member in (w_qkv, b_qkv, w_proj, b_proj, ln1_gain, ln1_shift, ln2_gain, ln2_shift, w_fc1, b_fc1, w_fc2, b_fc2)))

    def one_clip(totals, inputs):
        clip_tokens, clip_places, clip_cotangent = inputs
        cosine_table, sine_table = rotary_tables(clip_places, HD, ROT_PAIRS)

        def forward(token_values, weight_values):
            return block_forward(token_values, cosine_table, sine_table, weight_values)
        result, pullback = jax.vjp(forward, clip_tokens.astype(jnp.float32), weights)
        grad_tokens, grad_weights = pullback(clip_cotangent.astype(jnp.float32))
        totals = jax.tree.map(lambda summed, update: summed + update, totals, grad_weights)
        return (totals, (result.astype(jnp.bfloat16), grad_tokens.astype(jnp.bfloat16)))
    zero_grads = jax.tree.map(jnp.zeros_like, weights)
    totals, (outputs, grad_in) = lax.scan(one_clip, zero_grads, (tokens, jnp.moveaxis(places, 1, 0), d_out))
    return (outputs, grad_in, totals[0], totals[1], totals[2], totals[3], totals[4], totals[5], totals[6], totals[7], totals[8], totals[9], totals[10], totals[11])
```

```python
import math

import jax
import jax.numpy as jnp
from jax import lax
from jax.sharding import Mesh
from jax.sharding import PartitionSpec as P

HD = 64
ROT_PAIRS = 10
EPS = 1e-06
F32 = jnp.float32
BF16 = jnp.bfloat16
SWAP = [(0, 1), (1, 0)]


def dot(a, b, dims=((1,), (0,))):
    return lax.dot_general(a, b, (dims, ((), ())), preferred_element_type=F32)


def shift(values, amount, count):
    return lax.ppermute(values, "tp", [(i, (i + amount) % count) for i in range(count)])


def norm_stats(values):
    mean = jnp.mean(values, axis=-1, keepdims=True)
    centre = values - mean
    spread = jnp.mean(centre * centre, axis=-1, keepdims=True)
    return centre, lax.rsqrt(spread + EPS)


def norm_back(values, gain, cotangent):
    centre, scale = norm_stats(values)
    unit = centre * scale
    weighted = cotangent * gain
    back = scale * (
        weighted
        - jnp.mean(weighted, axis=-1, keepdims=True)
        - unit * jnp.mean(weighted * unit, axis=-1, keepdims=True)
    )
    return back, jnp.sum(cotangent * unit, axis=0), jnp.sum(cotangent, axis=0)


def turn(values):
    width = values.shape[1]
    row = lax.broadcasted_iota(jnp.int32, (width, width), 0)
    col = lax.broadcasted_iota(jnp.int32, (width, width), 1)
    sign = jnp.where(col % 2 == 0, -1.0, 1.0)
    pairs = jnp.where(row == (col ^ 1), sign, 0.0).astype(F32)
    return lax.dot(values, pairs, precision=lax.Precision.HIGHEST)


def rotary_tables(place_rows, heads):
    lane = jnp.arange(HD)
    portion = lane // (2 * ROT_PAIRS)
    within = lane % (2 * ROT_PAIRS) // 2
    frequency = jnp.exp(within.astype(F32) * (-math.log(10000.0) / ROT_PAIRS))
    angles = jnp.zeros((place_rows.shape[1], HD), F32)
    for component in range(3):
        picked = jnp.where(portion == component, frequency, jnp.zeros_like(frequency))
        angles = angles + place_rows[component].astype(F32)[:, None] * picked[None, :]
    return jnp.tile(jnp.cos(angles), (1, heads)), jnp.tile(jnp.sin(angles), (1, heads))


def make_body(owners, tp):
    def from_owners(piece):
        if owners == 2:
            mine = lax.axis_index("fsdp")
            other = lax.ppermute(piece, "fsdp", SWAP)
            return jnp.stack((jnp.where(mine == 0, piece, other), jnp.where(mine == 0, other, piece)))
        return lax.all_gather(piece, "fsdp", axis=0)

    def to_owners(stacked):
        if owners == 2:
            mine = lax.axis_index("fsdp")
            keep = lax.dynamic_index_in_dim(stacked, mine, 0, keepdims=False)
            send = lax.dynamic_index_in_dim(stacked, 1 - mine, 0, keepdims=False)
            return keep + lax.ppermute(send.astype(BF16), "fsdp", SWAP).astype(F32)
        return lax.psum_scatter(stacked.astype(BF16), "fsdp", scatter_dimension=0).astype(F32)

    def pick(core, first, second):
        return jnp.where(core == 0, first, second)

    def gather_rows(shard):
        core = lax.axis_index("cc")
        rows = shard.shape[0] // 2
        if owners == 2:
            mine = lax.axis_index("fsdp")
            send = lax.dynamic_slice_in_dim(shard, core * rows, rows, 0)
            near = lax.ppermute(send, "fsdp", SWAP)
            far = lax.ppermute(near, "cc", SWAP)
            other = jnp.concatenate((pick(core, near, far), pick(core, far, near)), axis=0)
            return jnp.stack((pick(mine, shard, other), pick(mine, other, shard)))
        send = lax.dynamic_slice_in_dim(shard, core * rows, rows, 0)
        near = lax.all_gather(send, "fsdp", axis=0)
        far = lax.ppermute(near, "cc", SWAP)
        return jnp.concatenate((pick(core, near, far), pick(core, far, near)), axis=1)

    def reduce_grad(split):
        core = lax.axis_index("cc")
        keep = lax.dynamic_index_in_dim(split, core, 0, keepdims=False)
        send = lax.dynamic_index_in_dim(split, 1 - core, 0, keepdims=False)
        both = keep + lax.ppermute(send.astype(BF16), "cc", SWAP).astype(F32)
        return to_owners(both)

    def finish_grad(part):
        core = lax.axis_index("cc")
        low = part.astype(BF16)
        summed = (low.astype(F32) + lax.ppermute(low, "cx", SWAP).astype(F32)).astype(BF16)
        far = lax.ppermute(summed, "cc", SWAP)
        return jnp.stack((pick(core, summed, far), pick(core, far, summed))).astype(F32)

    def scatter_tp(partial):
        rows = partial.shape[0] // tp
        total = partial[:rows]
        order = sorted(range(1, tp), key=lambda j: abs(j - tp / 2))
        got = [shift(partial[j * rows : (j + 1) * rows].astype(BF16), j, tp) for j in order]
        for piece in got:
            total = total + piece.astype(F32)
        return total

    def body(
        tokens,
        places,
        d_out,
        w_qkv,
        b_qkv,
        w_proj,
        b_proj,
        ln1_gain,
        ln1_shift,
        ln2_gain,
        ln2_shift,
        w_fc1,
        b_fc1,
        w_fc2,
        b_fc2,
    ):
        core = lax.axis_index("cc")
        z = lax.axis_index("tp")
        width = tokens.shape[2]
        local_len = tokens.shape[1]
        length = 2 * local_len
        heads = w_qkv.shape[2] // HD
        feat = heads * HD
        hidden = w_fc1.shape[1]
        chunk = length // tp

        def own_clip(values, axis, row_axis):
            keep = lax.dynamic_index_in_dim(values, core, axis, keepdims=False)
            send = lax.dynamic_index_in_dim(values, 1 - core, axis, keepdims=False)
            got = lax.ppermute(send, "cc", SWAP)
            doubled = jnp.concatenate((keep, got, keep, got), axis=row_axis)
            return lax.dynamic_slice_in_dim(doubled, z * chunk, length, row_axis)

        x = own_clip(tokens, 0, 0).astype(F32)
        place_rows = own_clip(places, 1, 1)
        cot = own_clip(d_out, 0, 0)

        flat = [b_qkv, b_proj, ln1_gain, ln1_shift, ln2_gain, ln2_shift, b_fc1, b_fc2]
        sizes = [v.size for v in flat]
        small = from_owners(jnp.concatenate([v.reshape(-1) for v in flat])).astype(F32)
        offsets = [sum(sizes[:i]) for i in range(len(sizes))]
        parts = [small[:, o : o + n] for o, n in zip(offsets, sizes)]
        bias_qkv = jnp.moveaxis(parts[0].reshape((owners,) + b_qkv.shape), 0, 2).reshape(3, 1, feat)
        bias_proj, gain1, shift1, gain2, shift2 = [p.reshape(1, width) for p in parts[1:6]]
        bias_fc1 = jnp.moveaxis(parts[6].reshape((owners,) + b_fc1.shape), 0, 1).reshape(1, hidden)
        bias_fc2 = parts[7].reshape(1, width)

        own_rows = w_qkv.shape[1]
        qkv = gather_rows(jnp.moveaxis(w_qkv, 0, 1).reshape(own_rows, 3 * feat)).reshape(width, 3 * feat)
        w_q, w_k, w_v = (qkv[:, j * feat : (j + 1) * feat] for j in range(3))

        cosine, sine = rotary_tables(place_rows, heads)
        centre1, scale1 = norm_stats(x)
        h1 = (centre1 * scale1 * gain1 + shift1).astype(BF16)

        def rotated(pre):
            return pre * cosine + turn(pre) * sine

        def rotated_back(grad):
            return grad * cosine - turn(grad) * sine

        k = rotated(dot(h1, w_k) + bias_qkv[1]).astype(BF16)
        k_far = lax.ppermute(k, "cx", SWAP)
        v = (dot(h1, w_v) + bias_qkv[2]).astype(BF16)
        v_far = lax.ppermute(v, "cx", SWAP)
        q = (rotated(dot(h1, w_q) + bias_qkv[0]) * (1.0 / math.sqrt(HD))).astype(BF16)

        half = w_proj.shape[0] // 2
        sub = lax.dynamic_slice_in_dim(w_proj, core * half, half, 0)
        sub = jnp.moveaxis(from_owners(sub), 0, 1).reshape(half, width)
        subs = jnp.stack([sub] + [shift(sub, s, tp) for s in range(1, tp)])
        subs_far = lax.ppermute(subs, "cc", SWAP)
        proj = jnp.concatenate((pick(core, subs, subs_far), pick(core, subs_far, subs)), axis=1)

        fc1 = gather_rows(w_fc1).reshape(width, hidden)
        fc2 = jnp.moveaxis(gather_rows(w_fc2), 0, 1).reshape(hidden, width)

        lane_head = lax.broadcasted_iota(jnp.int32, (1, feat), 1) // HD
        head_mask = (lane_head == jnp.arange(heads)[:, None])[:, None, :]

        def by_head(values):
            return jnp.where(head_mask, values[None], jnp.zeros_like(values)[None]).reshape(heads * length, feat)

        def join_heads(values):
            return jnp.sum(jnp.where(head_mask, values.reshape(heads, length, feat), 0.0), axis=0)

        NT = ((1,), (1,))
        TN = ((0,), (0,))
        q_heads = by_head(q)
        s_near = dot(q_heads, k, NT)
        s_far = dot(q_heads, k_far, NT)
        row_max = jnp.maximum(jnp.max(s_near, axis=-1, keepdims=True), jnp.max(s_far, axis=-1, keepdims=True))
        e_near = jnp.exp(s_near - row_max)
        e_far = jnp.exp(s_far - row_max)
        inverse = 1.0 / (jnp.sum(e_near, axis=-1, keepdims=True) + jnp.sum(e_far, axis=-1, keepdims=True))
        p_near = (e_near * inverse).astype(BF16)
        p_far = (e_far * inverse).astype(BF16)
        a = join_heads(dot(p_near, v) + dot(p_far, v_far)).astype(BF16)

        d_active = dot(cot, fc2, NT)

        pieces = [a] + [
            jnp.concatenate((g[s * chunk :], g[: s * chunk]), axis=0)
            for s, g in ((s, shift(a, s, tp)) for s in range(1, tp))
        ]
        x2 = x + bias_proj
        for s in range(tp):
            x2 = x2 + dot(pieces[s], proj[s])
        centre2, scale2 = norm_stats(x2)
        h2 = (centre2 * scale2 * gain2 + shift2).astype(BF16)

        u = dot(h2, fc1) + bias_fc1
        phi = 0.5 * (1.0 + lax.erf(u * math.sqrt(0.5)))
        g = (u * phi).astype(BF16)
        slope = phi + u * jnp.exp(-0.5 * u * u) * (1.0 / math.sqrt(2.0 * math.pi))
        du = (d_active * slope).astype(BF16)
        dh2 = scatter_tp(dot(du, fc1, NT))
        part_out = dot(g, fc2)

        cot_own = cot[:chunk].astype(F32)
        back2, grad_gain2, grad_shift2 = norm_back(x2[:chunk], gain2, dh2)
        dx2 = cot_own + back2
        db = dx2.astype(BF16)

        da_pieces = [dot(db, proj[s], NT).astype(BF16) for s in range(tp)]
        da = jnp.concatenate([da_pieces[0]] + [shift(da_pieces[s], -s, tp) for s in range(1, tp)], axis=0)

        da_heads = by_head(da)
        inner = jnp.sum(
            jnp.where(head_mask, (a.astype(F32) * da.astype(F32))[None], 0.0), axis=-1, keepdims=True
        ).reshape(heads * length, 1)

        def d_scores(p, values):
            return (p.astype(F32) * (dot(da_heads, values, NT) - inner)).astype(BF16)

        ds_far = d_scores(p_far, v_far)
        dk_send = dot(ds_far, q_heads, TN).astype(BF16)
        dk_got = lax.ppermute(dk_send, "cx", SWAP)
        dv_send = dot(p_far, da_heads, TN).astype(BF16)
        dv_got = lax.ppermute(dv_send, "cx", SWAP)
        ds_near = d_scores(p_near, v)
        dq = join_heads(dot(ds_near, k) + dot(ds_far, k_far)) * (1.0 / math.sqrt(HD))
        d0 = rotated_back(dq).astype(BF16)
        dk = dot(ds_near, q_heads, TN) + dk_got.astype(F32)
        d1 = rotated_back(dk).astype(BF16)
        d2 = (dot(p_near, da_heads, TN) + dv_got.astype(F32)).astype(BF16)
        d_all = jnp.concatenate((d0, d1, d2), axis=1)
        dh1 = scatter_tp(dot(d_all, qkv, NT))

        own_out = (x2[:chunk] + scatter_tp(part_out) + bias_fc2).astype(BF16)
        back1, grad_gain1, grad_shift1 = norm_back(x[:chunk], gain1, dh1)
        own_dx = (dx2 + back1).astype(BF16)

        def spread(own):
            rows = jnp.zeros((length, width), BF16)
            rows = lax.dynamic_update_slice_in_dim(rows, own, z * chunk, 0)
            for j in range(1, tp):
                rows = lax.dynamic_update_slice_in_dim(rows, shift(own, -j, tp), ((z + j) % tp) * chunk, 0)
            mine, theirs = rows[:local_len], rows[local_len:]
            got = lax.ppermute(theirs, "cc", SWAP)
            return jnp.stack((pick(core, mine, got), pick(core, got, mine)))

        own = width // owners
        g_fc2 = dot(g, cot, TN).reshape(2, hidden // 2, owners, own)
        g_fc1 = dot(h2, du, TN).reshape(owners, 2, own // 2, hidden)
        g_qkv = dot(h1, d_all, TN).reshape(owners, 2, own // 2, 3 * feat)
        own_fc2 = finish_grad(reduce_grad(jnp.moveaxis(g_fc2, 2, 1)))
        own_fc1 = finish_grad(reduce_grad(jnp.moveaxis(g_fc1, 1, 0)))
        own_qkv = finish_grad(reduce_grad(jnp.moveaxis(g_qkv, 1, 0)))

        g_proj = jnp.stack([dot(pieces[s][:chunk], db, TN).reshape(2, feat // 2, owners, own) for s in range(tp)])
        r_proj = reduce_grad(g_proj.transpose(1, 3, 0, 2, 4))
        t_proj = r_proj[0]
        for s in range(1, tp):
            t_proj = t_proj + shift(r_proj[s].astype(BF16), -s, tp).astype(F32)
        own_proj = finish_grad(t_proj)

        common = jnp.concatenate(
            (jnp.sum(cot_own, axis=0), jnp.sum(db.astype(F32), axis=0), grad_gain1, grad_shift1, grad_gain2, grad_shift2)
        )
        step = 1
        while step < tp:
            common = common + lax.ppermute(common, "tp", [(i, i ^ step) for i in range(tp)])
            step *= 2
        vector = jnp.concatenate(
            (common, jnp.sum(du.astype(F32), axis=0), jnp.sum(d_all.astype(F32), axis=0))
        )
        vector = vector + lax.ppermute(vector, "cc", SWAP)
        vector = vector + lax.ppermute(vector, "cx", SWAP)
        if owners == 2:
            vector = vector + lax.ppermute(vector, "fsdp", SWAP)
        else:
            vector = lax.psum(vector, "fsdp")
        fs = lax.axis_index("fsdp")

        def mine_of(values, axis):
            size = values.shape[axis] // owners
            return lax.dynamic_slice_in_dim(values, fs * size, size, axis)

        s_bfc2, s_bproj, s_g1, s_s1, s_g2, s_s2 = (
            mine_of(vector[i * width : (i + 1) * width], 0) for i in range(6)
        )
        s_bfc1 = mine_of(vector[6 * width : 6 * width + hidden].reshape(b_fc1.shape[0], -1), 1)
        s_bqkv = mine_of(vector[6 * width + hidden :].reshape(3, heads, HD), 2)

        return (
            spread(own_out),
            spread(own_dx),
            jnp.moveaxis(own_qkv.reshape(own, 3, feat), 1, 0),
            s_bqkv,
            own_proj.reshape(feat, own),
            s_bproj,
            s_g1,
            s_s1,
            s_g2,
            s_s2,
            own_fc1.reshape(own, hidden),
            s_bfc1,
            own_fc2.reshape(hidden, own),
            s_bfc2,
        )

    return body


def solution(mesh):
    owners, ctx, tp = mesh.devices.shape
    paired = Mesh(mesh.devices.reshape(owners, ctx // 2, 2, tp), ("fsdp", "cx", "cc", "tp"))
    ctx_axes = ("cx", "cc")
    placed = (
        P("fsdp", ctx_axes, None),
        P(None, "fsdp", ctx_axes),
        P("fsdp", ctx_axes, None),
        P(None, "fsdp", "tp"),
        P(None, "tp", "fsdp"),
        P("tp", "fsdp"),
        P("fsdp"),
        P("fsdp"),
        P("fsdp"),
        P("fsdp"),
        P("fsdp"),
        P("fsdp", "tp"),
        P("tp", "fsdp"),
        P("tp", "fsdp"),
        P("fsdp"),
    )
    return jax.shard_map(
        make_body(owners, tp),
        mesh=paired,
        in_specs=placed,
        out_specs=(
            P("fsdp", ctx_axes, None),
            P("fsdp", ctx_axes, None),
            P(None, "fsdp", "tp"),
            P(None, "tp", "fsdp"),
            P("tp", "fsdp"),
            P("fsdp"),
            P("fsdp"),
            P("fsdp"),
            P("fsdp"),
            P("fsdp"),
            P("fsdp", "tp"),
            P("tp", "fsdp"),
            P("tp", "fsdp"),
            P("fsdp"),
        ),
        check_vma=False,
    )
```
